32 devices in a mesh: row: 8 (over y, x, core), col: 4 (over z).
Axes of the slice: x: 2, y: 2, z: 4, core: 2. Of those that a mesh axis runs over, the one named last changes fastest.
Arguments:
- columns: float32 [16384, 1024], P('row', 'col'), as said below
Outputs:
- factored: float32 [16384, 1024], P('row', 'col')
- projected: float32 [256, 1024], P(None, 'col')
Inputs may be any that keep to these rules, and one draw needn't show every extreme that they name: `columns`: the panel has full column rank and a condition number of at most about 40.
All inputs are finite; a program needn't handle non-finite values.
Results may differ from the reference program's by a relative error of at most 0.0003.
Values sent between devices are 32-bit elements; how exact they have to be, the bound alone decides.
No kernel may reach another device: no remote copies, remote signals or barrier semaphores. Data moves between devices by JAX's collectives and lax.ppermute only.
A program may use at most 64 MiB of HBM per device.

```python
import math
import jax
import jax.numpy as jnp
from jax import lax

NB = 256
M = 16384
COLS = 1024


def draw_columns(key, part):
    keys = jax.random.split(key, 9)
    position = jnp.arange(M, dtype=jnp.float32)[:, None] / M
    row_scale = jnp.exp(position * math.log(3.0)) * jnp.exp(jax.random.uniform(keys[0], (M, 1), jnp.float32) * math.log(3.0))
    col_scale = jnp.exp(jax.random.uniform(keys[1], (1, NB), jnp.float32) * math.log(2.0))
    linked = max(NB // 16, 1)
    free_count = NB - linked
    order = jax.random.permutation(keys[6], NB)
    first_pick = jax.random.randint(keys[7], (linked,), 0, free_count)
    second_pick = (first_pick + 1 + jax.random.randint(keys[8], (linked,), 0, free_count - 1)) % free_count
    first_cols = order[first_pick]
    second_cols = order[second_pick]
    tied_cols = order[free_count:]
    tied_hot = jax.nn.one_hot(tied_cols, NB, dtype=jnp.float32)
    first_hot = jax.nn.one_hot(first_cols, NB, dtype=jnp.float32)
    second_hot = jax.nn.one_hot(second_cols, NB, dtype=jnp.float32)
    tied_mask = jnp.sum(tied_hot, axis=0)
    nudge = 0.35
    noise = jax.random.normal(keys[2], (M, NB), jnp.float32)
    trailing = jax.random.normal(keys[5], (M, COLS - NB), jnp.float32)
    mixing = jnp.diag(1.0 - tied_mask + nudge * tied_mask)
    mixing = mixing + jnp.dot(0.6 * first_hot.T, tied_hot, precision=lax.Precision.HIGHEST)
    mixing = mixing + jnp.dot(0.8 * second_hot.T, tied_hot, precision=lax.Precision.HIGHEST)
    panel_base = jnp.dot(noise, mixing, precision=lax.Precision.HIGHEST, preferred_element_type=jnp.float32)
    panel_part = panel_base * row_scale * col_scale / (3.0 * math.sqrt(M))
    return jnp.concatenate([panel_part, trailing], axis=1).astype(jnp.float32)


def setup_inputs(seed: int = 0) -> dict:
    seeds = jax.random.split(jax.random.key(seed), 2)
    return {
        "columns": draw_columns(jax.random.fold_in(seeds[1], 71), 0),
    }


def reference(columns):
    panel_block = columns[:, :NB]
    basis, upper = jnp.linalg.qr(panel_block)
    sign_flip = jnp.where(jnp.diagonal(upper) < 0, -1.0, 1.0).astype(panel_block.dtype)
    basis = basis * sign_flip[None, :]
    projected = jnp.dot(basis.T.astype(jnp.float32), columns.astype(jnp.float32), precision=lax.Precision.HIGHEST, preferred_element_type=jnp.float32)
    trailing = columns[:, NB:] - jnp.dot(basis.astype(jnp.float32), projected[:, NB:].astype(jnp.float32), precision=lax.Precision.HIGHEST, preferred_element_type=jnp.float32)
    factored = jnp.concatenate([basis, trailing], axis=1)
    return (factored, projected)
```

```python
import jax
import jax.numpy as jnp
from jax import lax
from jax.sharding import PartitionSpec as P

CHUNKS = 8
HIGH = lax.Precision.HIGH
HIGHEST = lax.Precision.HIGHEST


def cross(left, right, precision):
    return lax.dot_general(
        left, right, (((0,), (0,)), ((), ())), precision=precision, preferred_element_type=jnp.float32
    )


def mul(left, right, precision):
    return jnp.dot(left, right, precision=precision, preferred_element_type=jnp.float32)


def hops(value, at, count):
    mid = count // 2
    first = lax.ppermute(value, "col", [(0, mid)])
    got = first
    held = None
    for step in range(1, mid + 1):
        up, down = (mid + step - 1, mid + step), (mid - step + 1, mid - step)
        pairs = [p for p in (up, down) if 0 < p[1] < count]
        if not pairs:
            break
        if step == 1:
            parts = [lax.ppermute(first, "col", [p]) for p in pairs]
            held = sum(parts[1:], parts[0])
        else:
            held = lax.ppermute(held, "col", pairs)
        got = got + held
    return got


def exchange_sum(value, count):
    index = lax.axis_index("row")
    half = value.shape[0] // 2
    odd = index % 2 == 1
    pairs = lambda bit: [(i, i ^ bit) for i in range(count)]
    low, high = value[:half], value[half:]
    mine = jnp.where(odd, high, low)
    mine = mine + lax.ppermute(jnp.where(odd, low, high), "row", pairs(1))
    bit = 2
    while bit < count:
        mine = mine + lax.ppermute(mine, "row", pairs(bit))
        bit *= 2
    other = lax.ppermute(mine, "row", pairs(1))
    return jnp.concatenate([jnp.where(odd, other, mine), jnp.where(odd, mine, other)], axis=0)


def invert_lower(gram):
    lower = jnp.linalg.cholesky(gram)
    ident = jnp.eye(gram.shape[0], dtype=jnp.float32)
    return jax.scipy.linalg.solve_triangular(lower, ident, lower=True)


def solution(mesh):
    rows, cols = mesh.shape["row"], mesh.shape["col"]

    def per_device(columns):
        at = lax.axis_index("col")
        root = at == 0
        size = columns.shape[0] // CHUNKS
        own = [columns[k * size : (k + 1) * size] for k in range(CHUNKS)]
        got = [hops(c, at, cols) for c in own]
        gram = exchange_sum(cross(columns, columns, HIGH), rows)
        inverse = invert_lower(gram)
        inverse = jnp.where(root, inverse, hops(inverse, at, cols))
        panel = [jnp.where(root, o, g) for o, g in zip(own, got)]
        partial = sum(cross(p, o, HIGH) for p, o in zip(panel, own))
        total = exchange_sum(partial, rows)
        projected = mul(inverse, total, HIGHEST)
        weight = jnp.where(root, -inverse.T, mul(inverse.T, projected, HIGHEST))
        out = [jnp.where(root, 0.0, o) - mul(p, weight, HIGH) for p, o in zip(panel, own)]
        return (jnp.concatenate(out, axis=0), projected)

    return jax.shard_map(
        per_device, mesh=mesh, in_specs=(P("row", "col"),), out_specs=(P("row", "col"), P(None, "col")), check_vma=False
    )
```

```python
import jax
import jax.numpy as jnp
from jax import lax
from jax.experimental import pallas as pl
from jax.experimental.pallas import tpu as pltpu
from jax.sharding import PartitionSpec as P


CHUNKS = 8
GROUPS = ((0, 1, 2, 3), (4, 5, 6), (7,))
TILE = 64
F32 = jnp.float32
BF16 = jnp.bfloat16
VMEM = pl.BlockSpec(memory_space=pltpu.VMEM)
SMEM = pl.BlockSpec(memory_space=pltpu.SMEM)
ANY = pl.BlockSpec(memory_space=pl.ANY)
NN = ((1,), (0,))
TN = ((0,), (0,))


def fine(left, right, dims=NN):
    return lax.dot_general(left, right, (dims, ((), ())), precision=lax.Precision.HIGHEST, preferred_element_type=F32)


def split(value):
    high = value.astype(BF16)
    return high, (value - high.astype(F32)).astype(BF16)


def three(left, right, dims=NN):
    one = lambda a, b: lax.dot_general(a, b, (dims, ((), ())), preferred_element_type=F32)
    return one(left[0], right[0]) + (one(left[0], right[1]) + one(left[1], right[0]))


def gram_kernel(block_ref, out_ref):
    pair = split(block_ref[...])
    part = three(pair, pair, TN)

    @pl.when(pl.program_id(0) == 0)
    def _():
        out_ref[...] = part

    @pl.when(pl.program_id(0) > 0)
    def _():
        out_ref[...] += part


def gram_of(columns):
    rows, width = columns.shape
    step = rows // CHUNKS
    return pl.pallas_call(
        gram_kernel,
        out_shape=jax.ShapeDtypeStruct((width, width), F32),
        grid=(CHUNKS,),
        in_specs=[pl.BlockSpec((step, width), lambda k: (k, 0))],
        out_specs=pl.BlockSpec((width, width), lambda k: (0, 0)),
        name="gram",
    )(columns)


def eliminate(tile, size):
    lanes = tile.shape[1]
    row = lax.broadcasted_iota(jnp.int32, (size, 1), 0)
    for j in range(0, size, 2):
        low = j // 8 * 8
        tail, at = tile[low:], row[low:]
        k, count = j - low, size - low
        c0 = jnp.broadcast_to(tail[:, j : j + 1], (count, lanes))
        c1 = jnp.broadcast_to(tail[:, j + 1 : j + 2], (count, lanes))
        p00, p01, p11 = c0[k : k + 1], c1[k : k + 1], c1[k + 1 : k + 2]
        r0, r1 = tail[k : k + 1], tail[k + 1 : k + 2]
        scale = 1.0 / (p00 * p11 - p01 * p01)
        q0 = (p11 * r0 - p01 * r1) * scale
        q1 = (p00 * r1 - p01 * r0) * scale
        inner = r0 * (p01 * (1.0 / p00))
        tail = tail - jnp.where(at > j + 1, c0 * q0 + c1 * q1, jnp.where(at == j + 1, inner, 0.0))
        tile = tail if low == 0 else jnp.concatenate([tile[:low], tail], axis=0)
    return tile


def identity(size):
    shape = (size, size)
    same = lax.broadcasted_iota(jnp.int32, shape, 0) == lax.broadcasted_iota(jnp.int32, shape, 1)
    return jnp.where(same, 1.0, 0.0).astype(F32)


def factor_kernel(flag_ref, gram_ref, out_ref, work_ref):
    width = gram_ref.shape[0]

    @pl.when(flag_ref[0] == 1)
    def _():
        work_ref[:, :width] = gram_ref[...]
        work_ref[:, width:] = identity(width)
        eye = identity(TILE)
        for start in range(0, width, TILE):
            end = start + TILE
            tile = jnp.concatenate([work_ref[start:end, start:end], eye], axis=1)
            tile = eliminate(tile, TILE)
            pivots = jnp.sum(tile[:, :TILE] * eye, axis=1, keepdims=True)
            block = fine(tile[:, TILE:] * lax.rsqrt(pivots), work_ref[start:end, :])
            work_ref[start:end, :] = block
            if end < width:
                work_ref[end:, :] = work_ref[end:, :] - fine(block[:, end:width], block, TN)
        out_ref[...] = work_ref[:, width:]


def inverse_of(flag, gram):
    width = gram.shape[0]
    return pl.pallas_call(
        factor_kernel,
        out_shape=jax.ShapeDtypeStruct((width, width), F32),
        in_specs=[SMEM, VMEM],
        out_specs=VMEM,
        scratch_shapes=[pltpu.VMEM((width, 2 * width), F32)],
        name="factor",
    )(flag, gram)


def gather_kernel(first, count, hops, step, flag_ref, *refs):
    columns_ref, before_ref = refs[:2]
    moved = refs[2 : 2 + count * hops]
    sum_ref, high_ref, low_ref = refs[2 + count * hops :]
    total = before_ref[...] if first > 0 else None
    for c in range(count):
        block = columns_ref[(first + c) * step : (first + c + 1) * step, :]
        parts = [ref[...] for ref in moved[c * hops : (c + 1) * hops]]
        got = sum(parts[1:], parts[0]) if parts else block
        pair = split(jnp.where(flag_ref[0] == 1, block, got))
        high_ref[c * step : (c + 1) * step, :] = pair[0]
        low_ref[c * step : (c + 1) * step, :] = pair[1]
        part = three(pair, split(block), TN)
        total = part if total is None else total + part
    sum_ref[...] = total


def gather(flag, columns, before, moved, first):
    count, hops, step = len(moved), len(moved[0]), columns.shape[0] // CHUNKS
    width = columns.shape[1]
    flat = [m for ms in moved for m in ms]
    return pl.pallas_call(
        lambda *refs: gather_kernel(first, count, hops, step, *refs),
        out_shape=(
            jax.ShapeDtypeStruct((width, width), F32),
            jax.ShapeDtypeStruct((count * step, width), BF16),
            jax.ShapeDtypeStruct((count * step, width), BF16),
        ),
        in_specs=[SMEM] + [VMEM] * (2 + len(flat)),
        out_specs=(VMEM, VMEM, VMEM),
    )(flag, columns, before, *flat)


def finish_kernel(groups, hops, flag_ref, own_ref, gram_ref, total_ref, columns_ref, *refs):
    moved = refs[:hops]
    pairs = refs[hops : hops + 2 * len(groups)]
    out_ref, projected_ref, buffer_ref, sem = refs[hops + 2 * len(groups) :]
    root = flag_ref[0] == 1
    got = own_ref[...]
    if hops:
        parts = [ref[...] for ref in moved]
        got = jnp.where(root, got, sum(parts[1:], parts[0]))
    projected = fine(got, jnp.where(root, gram_ref[...], total_ref[...]))
    projected_ref[...] = projected
    weight = split(jnp.where(root, -got.T, fine(got, projected, TN)))
    step = columns_ref.shape[0] // CHUNKS
    copies = []
    for g, group in enumerate(groups):
        for c, chunk in enumerate(group):
            here = pl.ds(c * step, step)
            there = pl.ds(chunk * step, step)
            pair = (pairs[2 * g][here, :], pairs[2 * g + 1][here, :])
            base = jnp.where(root, 0.0, columns_ref[there, :])
            buffer_ref[there, :] = base - three(pair, weight)
            copies.append(pltpu.make_async_copy(buffer_ref.at[there, :], out_ref.at[there, :], sem.at[chunk]))
            copies[-1].start()
    for copy in copies:
        copy.wait()


def finish(flag, own, gram, total, columns, moved, pairs):
    rows, width = columns.shape
    return pl.pallas_call(
        lambda *refs: finish_kernel(GROUPS, len(moved), *refs),
        out_shape=(jax.ShapeDtypeStruct((rows, width), F32), jax.ShapeDtypeStruct((width, width), F32)),
        in_specs=[SMEM] + [VMEM] * (4 + len(moved) + len(pairs)),
        out_specs=(ANY, VMEM),
        scratch_shapes=[pltpu.VMEM((rows, width), F32), pltpu.SemaphoreType.DMA((CHUNKS,))],
        name="finish",
    )(flag, own, gram, total, columns, *moved, *pairs)


def exchange_sum(value, rows, cols, members):
    axes = ("row", "col")
    odd = lax.axis_index("row") % 2 == 1

    def swap(part, bit):
        pairs = [(r * cols + c, (r ^ bit) * cols + c) for r in range(rows) for c in members]
        return lax.ppermute(part, axes, pairs)

    half = value.shape[0] // 2
    low, high = value[:half], value[half:]
    mine = jnp.where(odd, high, low) + swap(jnp.where(odd, low, high), 1)
    bit = 2
    while bit < rows:
        mine = mine + swap(mine, bit)
        bit *= 2
    other = swap(mine, 1)
    return jnp.concatenate([jnp.where(odd, other, mine), jnp.where(odd, mine, other)], axis=0)


def spread(value, cols):
    mid = cols // 2
    held = lax.ppermute(value, "col", [(0, mid)])
    parts = [held]
    for step in range(1, mid + 1):
        pairs = [(mid + step - 1, mid + step), (mid - step + 1, mid - step)]
        pairs = [p for p in pairs if 0 < p[1] < cols]
        if not pairs:
            break
        if step == 1:
            sent = []
            for pair in pairs:
                sent.append(lax.ppermute(held, "col", [pair]))
            parts += sent
            held = sum(sent[1:], sent[0])
        else:
            held = lax.ppermute(held, "col", pairs)
            parts.append(held)
    return parts


def solution(mesh):
    rows, cols = mesh.shape["row"], mesh.shape["col"]

    def per_device(columns):
        step = columns.shape[0] // CHUNKS
        flag = (lax.axis_index("col") == 0).astype(jnp.int32).reshape(1)
        moved = [spread(columns[c * step : (c + 1) * step], cols) for c in range(CHUNKS)]
        gram = gram_of(columns)
        gram = exchange_sum(gram, rows, cols, (0,))
        inverse = inverse_of(flag, gram)
        sent = []
        for c in range(1, cols):
            sent.append(lax.ppermute(inverse, "col", [(0, c)]))
        total, pairs = gram, []
        for group in GROUPS:
            total, *pair = gather(flag, columns, total, [moved[c] for c in group], group[0])
            pairs += pair
        total = exchange_sum(total, rows, cols, tuple(range(1, cols)))
        return tuple(finish(flag, inverse, gram, total, columns, sent, pairs))

    return jax.shard_map(
        per_device, mesh=mesh, in_specs=(P("row", "col"),), out_specs=(P("row", "col"), P(None, "col")), check_vma=False
    )
```

```python
import jax
import jax.numpy as jnp
from jax import lax
from jax.experimental import pallas as pl
from jax.experimental.pallas import tpu as pltpu
from jax.sharding import PartitionSpec as P


PAIRS = 4
CHUNKS = 2 * PAIRS
TILE = 64
F32 = jnp.float32
BF16 = jnp.bfloat16
VMEM = pl.BlockSpec(memory_space=pltpu.VMEM)
SMEM = pl.BlockSpec(memory_space=pltpu.SMEM)
ANY = pl.BlockSpec(memory_space=pl.ANY)
NN = ((1,), (0,))
TN = ((0,), (0,))
ROOT, LOWER, _, ODD = range(4)


def kernel_call(body, ctrl, operands, outputs, scratch=(), hbm_in=0, hbm_out=0, room=8):
    held = [pltpu.with_memory_space_constraint(o, pltpu.VMEM) for o in operands[hbm_in:]]
    shapes = [jax.ShapeDtypeStruct(s, d) for s, d in outputs[:hbm_out]]
    shapes += [pltpu.VMEM(s, d) for s, d in outputs[hbm_out:]]
    return pl.pallas_call(
        body,
        out_shape=tuple(shapes),
        in_specs=[SMEM] + [ANY] * hbm_in + [VMEM] * len(held),
        out_specs=tuple([ANY] * hbm_out + [VMEM] * (len(outputs) - hbm_out)),
        scratch_shapes=scratch,
        compiler_params=pltpu.CompilerParams(vmem_limit_bytes=room << 20),
    )(ctrl, *[pltpu.with_memory_space_constraint(o, pltpu.HBM) for o in operands[:hbm_in]], *held)


def fine(left, right, dims=NN):
    return lax.dot_general(left, right, (dims, ((), ())), precision=lax.Precision.HIGHEST, preferred_element_type=F32)


def split(value):
    high = value.astype(BF16)
    return high, (value - high.astype(F32)).astype(BF16)


def three(left, right, dims=NN):
    one = lambda a, b: lax.dot_general(a, b, (dims, ((), ())), preferred_element_type=F32)
    return one(left[0], right[0]) + (one(left[0], right[1]) + one(left[1], right[0]))


def halves(value, ctrl_ref, keep_ref, send_ref):
    half = value.shape[0] // 2
    odd = ctrl_ref[ODD] == 1
    keep_ref[...] = jnp.where(odd, value[half:], value[:half])
    send_ref[...] = jnp.where(odd, value[:half], value[half:])


def joined(ctrl_ref, mine, other):
    odd = ctrl_ref[ODD] == 1
    return jnp.concatenate([jnp.where(odd, other, mine), jnp.where(odd, mine, other)], axis=0)


def load(ctrl, columns):
    rows, width = columns.shape
    step = rows // CHUNKS

    def body(ctrl_ref, columns_ref, *refs):
        outs, sem = refs[:CHUNKS], refs[CHUNKS]
        copies = [
            pltpu.make_async_copy(columns_ref.at[pl.ds(c * step, step), :], outs[c], sem.at[c]) for c in range(CHUNKS)
        ]
        for copy in copies:
            copy.start()
        for copy in copies:
            copy.wait()

    shape = [((step, width), F32)] * CHUNKS
    return kernel_call(body, ctrl, [columns], shape, [pltpu.SemaphoreType.DMA((CHUNKS,))], hbm_in=1)


def gram_halves(ctrl, chunks):
    width = chunks[0].shape[1]

    def body(ctrl_ref, *refs):
        ins, (keep_ref, send_ref) = refs[:CHUNKS], refs[CHUNKS:]

        @pl.when(ctrl_ref[ROOT] == 1)
        def _():
            total = None
            for ref in ins:
                pair = split(ref[...])
                part = three(pair, pair, TN)
                total = part if total is None else total + part
            halves(total, ctrl_ref, keep_ref, send_ref)

    return kernel_call(body, ctrl, chunks, [((width // 2, width), F32)] * 2)


def eliminate(tile, size):
    lanes = tile.shape[1]
    row = lax.broadcasted_iota(jnp.int32, (size, 1), 0)
    for j in range(0, size, 2):
        low = j // 8 * 8
        tail, at = tile[low:], row[low:]
        k, count = j - low, size - low
        c0 = jnp.broadcast_to(tail[:, j : j + 1], (count, lanes))
        c1 = jnp.broadcast_to(tail[:, j + 1 : j + 2], (count, lanes))
        p00, p01, p11 = c0[k : k + 1], c1[k : k + 1], c1[k + 1 : k + 2]
        r0, r1 = tail[k : k + 1], tail[k + 1 : k + 2]
        scale = 1.0 / (p00 * p11 - p01 * p01)
        q0 = (p11 * r0 - p01 * r1) * scale
        q1 = (p00 * r1 - p01 * r0) * scale
        inner = r0 * (p01 * (1.0 / p00))
        tail = tail - jnp.where(at > j + 1, c0 * q0 + c1 * q1, jnp.where(at == j + 1, inner, 0.0))
        tile = tail if low == 0 else jnp.concatenate([tile[:low], tail], axis=0)
    return tile


def identity(size):
    shape = (size, size)
    same = lax.broadcasted_iota(jnp.int32, shape, 0) == lax.broadcasted_iota(jnp.int32, shape, 1)
    return jnp.where(same, 1.0, 0.0).astype(F32)


def factor(ctrl, mine, other):
    width = mine.shape[1]

    def body(ctrl_ref, mine_ref, other_ref, gram_ref, inverse_ref, work_ref):
        @pl.when(ctrl_ref[ROOT] == 1)
        def _():
            gram = joined(ctrl_ref, mine_ref[...], other_ref[...])
            gram_ref[...] = gram
            work_ref[:, :width] = gram
            work_ref[:, width:] = identity(width)
            eye = identity(TILE)
            for start in range(0, width, TILE):
                end = start + TILE
                tile = jnp.concatenate([work_ref[start:end, start:end], eye], axis=1)
                tile = eliminate(tile, TILE)
                pivots = jnp.sum(tile[:, :TILE] * eye, axis=1, keepdims=True)
                block = fine(tile[:, TILE:] * lax.rsqrt(pivots), work_ref[start:end, :])
                work_ref[start:end, :] = block
                if end < width:
                    work_ref[end:, :] = work_ref[end:, :] - fine(block[:, end:width], block, TN)
            inverse_ref[...] = work_ref[:, width:]

    shape = [((width, width), F32)] * 2
    return kernel_call(body, ctrl, [mine, other], shape, [pltpu.VMEM((width, 2 * width), F32)])


def gather(ctrl, total, chunks, moved, last):
    step, width = chunks[0].shape
    first = total is None
    counts = [len(m) for m in moved[1:]]

    def body(ctrl_ref, *refs):
        refs = list(refs)
        sum_ref = None if first else refs.pop(0)
        blocks = [refs.pop(0)[...] for _ in range(2)]
        swapped = refs.pop(0)[...] if moved[0] else None
        parts = []
        for n in counts:
            got = [refs.pop(0)[...] for _ in range(n)]
            parts.append(sum(got[1:], got[0]) if got else None)
        outs = refs[:4]
        acc = None if first else sum_ref[...]
        for k in range(2):
            got = blocks[k]
            if parts[k] is not None:
                got = parts[k]
                if swapped is not None:
                    got = jnp.where(ctrl_ref[LOWER + k] == 1, swapped, got)
                got = jnp.where(ctrl_ref[ROOT] == 1, blocks[k], got)
            pair = split(got)
            outs[2 * k][...], outs[2 * k + 1][...] = pair
            part = three(pair, split(blocks[k]), TN)
            acc = part if acc is None else acc + part
        if last:
            halves(acc, ctrl_ref, *refs[4:])
        else:
            refs[4][...] = acc

    flat = ([] if first else [total]) + list(chunks) + [m for ms in moved for m in ms]
    shape = [((step, width), BF16)] * 4
    shape += [((width // 2, width), F32)] * 2 if last else [((width, width), F32)]
    return kernel_call(body, ctrl, flat, shape)


def finish(ctrl, inverse, gram, mine, other, chunks, sent, pairs):
    step, width = chunks[0].shape

    def body(ctrl_ref, own_ref, gram_ref, mine_ref, other_ref, *refs):
        blocks, refs = refs[:CHUNKS], refs[CHUNKS:]
        moved, refs = refs[: len(sent)], refs[len(sent) :]
        held, refs = refs[: 2 * CHUNKS], refs[2 * CHUNKS :]
        out_ref, projected_ref, buffer_ref, small_ref, sem = refs
        root = ctrl_ref[ROOT] == 1
        got = own_ref[...]
        if moved:
            parts = [ref[...] for ref in moved]
            got = jnp.where(root, got, sum(parts[1:], parts[0]))
        projected = fine(got, jnp.where(root, gram_ref[...], joined(ctrl_ref, mine_ref[...], other_ref[...])))
        small_ref[...] = projected
        copies = [pltpu.make_async_copy(small_ref, projected_ref, sem.at[CHUNKS])]
        copies[0].start()
        weight = split(jnp.where(root, -got.T, fine(got, projected, TN)))
        for c in range(CHUNKS):
            there = pl.ds(c * step, step)
            base = jnp.where(root, 0.0, blocks[c][...])
            buffer_ref[there, :] = base - three((held[2 * c][...], held[2 * c + 1][...]), weight)
            copies.append(pltpu.make_async_copy(buffer_ref.at[there, :], out_ref.at[there, :], sem.at[c]))
            copies[-1].start()
        for copy in copies:
            copy.wait()

    return kernel_call(
        body,
        ctrl,
        [inverse, gram, mine, other, *chunks, *sent, *pairs],
        [((CHUNKS * step, width), F32), ((width, width), F32)],
        [
            pltpu.VMEM((CHUNKS * step, width), F32),
            pltpu.VMEM((width, width), F32),
            pltpu.SemaphoreType.DMA((CHUNKS + 1,)),
        ],
        hbm_out=2,
        room=16,
    )


def added(ctrl, left, right):
    def body(ctrl_ref, left_ref, right_ref, out_ref):
        out_ref[...] = left_ref[...] + right_ref[...]

    return kernel_call(body, ctrl, [left, right], [(left.shape, F32)])[0]


def exchange(ctrl, mine, send, rows, cols, members):
    def swap(part, bit):
        pairs = [(r * cols + c, (r ^ bit) * cols + c) for r in range(rows) for c in members]
        return lax.ppermute(part, ("row", "col"), pairs)

    mine = added(ctrl, mine, swap(send, 1))
    bit = 2
    while bit < rows:
        mine = added(ctrl, mine, swap(mine, bit))
        bit *= 2
    return mine, swap(mine, 1)


def hop(value, pairs):
    return lax.ppermute(value, "col", pairs)


def spread(ctrl, chunks, cols):
    lower, upper = cols // 2, cols // 2 + 1
    two = cols > 3
    if not two:
        parts = [[hop(v, [(0, c)]) for c in range(1, cols)] for v in chunks]
        return [[], *parts]
    first = hop(chunks[0], [(0, upper)])
    second = hop(chunks[1], [(0, lower)])
    own = [(lower, lower - 1)] if lower > 1 else []
    far = [(upper, lower - 1)] if lower > 1 else []
    firsts, seconds = [first], [second]
    both = added(ctrl, first, second)
    swapped = hop(both, [(lower, upper), (upper, lower)])
    if upper + 1 < cols:
        near = hop(both, own + [(upper, upper + 1)])
        away = hop(both, far + [(lower, upper + 1)])
        above = lax.axis_index("col") > upper
        firsts.append(jnp.where(above, near, away))
        seconds.append(jnp.where(above, away, near))
        for tail, into in ((firsts[-1], firsts), (seconds[-1], seconds)):
            down, up = lower - 1, upper + 1
            while down > 1 or up + 1 < cols:
                pairs = ([(down, down - 1)] if down > 1 else []) + ([(up, up + 1)] if up + 1 < cols else [])
                tail = hop(tail, pairs)
                into.append(tail)
                down, up = down - 1, up + 1
    else:
        firsts.append(hop(first, far))
        seconds.append(hop(second, own))
    return [[swapped], firsts, seconds]


def solution(mesh):
    rows, cols = mesh.shape["row"], mesh.shape["col"]

    def per_device(columns):
        at = lax.axis_index("col")
        odd = lax.axis_index("row") % 2 == 1
        ctrl = jnp.stack([at == 0, at == cols // 2, at == cols // 2 + 1, odd]).astype(jnp.int32)
        chunks = load(ctrl, columns)
        moved = [spread(ctrl, chunks[2 * p : 2 * p + 2], cols) for p in range(PAIRS)]
        gram, inverse = factor(ctrl, *exchange(ctrl, *gram_halves(ctrl, chunks), rows, cols, (0,)))
        sent = [hop(inverse, [(0, c)]) for c in range(1, cols)]
        total, pairs = None, []
        for p in range(PAIRS):
            *held, total = gather(ctrl, total, chunks[2 * p : 2 * p + 2], moved[p], False) if (
                p + 1 < PAIRS
            ) else (*gather(ctrl, total, chunks[2 * p : 2 * p + 2], moved[p], True), None)
            pairs += held
        mine, send = pairs[2 * CHUNKS :]
        total = exchange(ctrl, mine, send, rows, cols, tuple(range(cols)))
        return tuple(finish(ctrl, inverse, gram, *total, chunks, sent, pairs[: 2 * CHUNKS]))

    return jax.shard_map(
        per_device, mesh=mesh, in_specs=(P("row", "col"),), out_specs=(P("row", "col"), P(None, "col")), check_vma=False
    )
```

```python
import jax
import jax.numpy as jnp
from jax import lax
from jax.experimental import pallas as pl
from jax.experimental.pallas import tpu as pltpu
from jax.sharding import PartitionSpec as P


PAIRS = 5
CHUNKS = 2 * PAIRS + 1
GROUPS = ((0, 1, 2, 3), (4, 5, 6, 7), (8, 9), (10,))
TILE = 64
F32 = jnp.float32
BF16 = jnp.bfloat16
VMEM = pl.BlockSpec(memory_space=pltpu.VMEM)
ANY = pl.BlockSpec(memory_space=pl.ANY)
NN = ((1,), (0,))
TN = ((0,), (0,))


def at_root():
    return lax.axis_index("col") == 0


def is_odd():
    return lax.axis_index("row") % 2 == 1


def kernel_call(body, operands, outputs, scratch=(), hbm_in=0, hbm_out=0, room=8):
    held = [pltpu.with_memory_space_constraint(o, pltpu.HBM) for o in operands[:hbm_in]]
    held += [pltpu.with_memory_space_constraint(o, pltpu.VMEM) for o in operands[hbm_in:]]
    shapes = [jax.ShapeDtypeStruct(s, d) for s, d in outputs[:hbm_out]]
    shapes += [pltpu.VMEM(s, d) for s, d in outputs[hbm_out:]]
    return pl.pallas_call(
        body,
        out_shape=tuple(shapes),
        in_specs=[ANY] * hbm_in + [VMEM] * (len(operands) - hbm_in),
        out_specs=tuple([ANY] * hbm_out + [VMEM] * (len(outputs) - hbm_out)),
        scratch_shapes=scratch,
        compiler_params=pltpu.CompilerParams(vmem_limit_bytes=room << 20),
    )(*held)


def fine(left, right, dims=NN):
    return lax.dot_general(left, right, (dims, ((), ())), precision=lax.Precision.HIGHEST, preferred_element_type=F32)


def split(value):
    high = value.astype(BF16)
    return high, (value - high.astype(F32)).astype(BF16)


def three(left, right, dims=NN):
    one = lambda a, b: lax.dot_general(a, b, (dims, ((), ())), preferred_element_type=F32)
    return one(left[0], right[0]) + (one(left[0], right[1]) + one(left[1], right[0]))


def halves(value, keep_ref, send_ref):
    half = value.shape[0] // 2
    odd = is_odd()
    keep_ref[...] = jnp.where(odd, value[half:], value[:half])
    send_ref[...] = jnp.where(odd, value[:half], value[half:])


def joined(mine, other):
    odd = is_odd()
    return jnp.concatenate([jnp.where(odd, other, mine), jnp.where(odd, mine, other)], axis=0)


def cuts(rows):
    step = -(-rows // (16 * CHUNKS)) * 16
    return [min(c * step, rows) for c in range(CHUNKS + 1)]


def fetch(columns_ref, refs, which, at, sem):
    copies = [
        pltpu.make_async_copy(columns_ref.at[at[c] : at[c + 1], :], ref, sem.at[k])
        for k, (c, ref) in enumerate(zip(which, refs))
    ]
    for copy in copies:
        copy.start()
    for copy in copies:
        copy.wait()


def head(columns):
    rows, width = columns.shape
    at = cuts(rows)

    def body(columns_ref, out_ref, sem):
        fetch(columns_ref, [out_ref], [0], at, sem)

    return kernel_call(body, [columns], [((at[1], width), F32)], [pltpu.SemaphoreType.DMA((1,))], hbm_in=1)[0]


def rest(columns, first):
    rows, width = columns.shape
    at = cuts(rows)
    others = list(range(1, CHUNKS))

    def body(columns_ref, first_ref, *refs):
        outs, (keep_ref, send_ref, sem) = refs[: len(others)], refs[len(others) :]
        fetch(columns_ref, outs, others, at, sem)

        @pl.when(at_root())
        def _():
            total = None
            for ref in (first_ref, *outs):
                pair = split(ref[...])
                part = three(pair, pair, TN)
                total = part if total is None else total + part
            halves(total, keep_ref, send_ref)

    shape = [((at[c + 1] - at[c], width), F32) for c in others] + [((width // 2, width), F32)] * 2
    return kernel_call(body, [columns, first], shape, [pltpu.SemaphoreType.DMA((len(others),))], hbm_in=1)


def eliminate(tile, size):
    lanes = tile.shape[1]
    row = lax.broadcasted_iota(jnp.int32, (size, 1), 0)
    for j in range(0, size, 2):
        low = j // 8 * 8
        tail, at = tile[low:], row[low:]
        k, count = j - low, size - low
        c0 = jnp.broadcast_to(tail[:, j : j + 1], (count, lanes))
        c1 = jnp.broadcast_to(tail[:, j + 1 : j + 2], (count, lanes))
        p00, p01, p11 = c0[k : k + 1], c1[k : k + 1], c1[k + 1 : k + 2]
        r0, r1 = tail[k : k + 1], tail[k + 1 : k + 2]
        scale = 1.0 / (p00 * p11 - p01 * p01)
        q0 = (p11 * r0 - p01 * r1) * scale
        q1 = (p00 * r1 - p01 * r0) * scale
        inner = r0 * (p01 * (1.0 / p00))
        tail = tail - jnp.where(at > j + 1, c0 * q0 + c1 * q1, jnp.where(at == j + 1, inner, 0.0))
        tile = tail if low == 0 else jnp.concatenate([tile[:low], tail], axis=0)
    return tile


def identity(size):
    shape = (size, size)
    same = lax.broadcasted_iota(jnp.int32, shape, 0) == lax.broadcasted_iota(jnp.int32, shape, 1)
    return jnp.where(same, 1.0, 0.0).astype(F32)


def factor(mine, other):
    width = mine.shape[1]

    def body(mine_ref, other_ref, gram_ref, inverse_ref, work_ref):
        @pl.when(at_root())
        def _():
            gram = joined(mine_ref[...], other_ref[...])
            gram_ref[...] = gram
            work_ref[:, :width] = gram
            work_ref[:, width:] = identity(width)
            eye = identity(TILE)
            for start in range(0, width, TILE):
                end = start + TILE
                tile = jnp.concatenate([work_ref[start:end, start:end], eye], axis=1)
                tile = eliminate(tile, TILE)
                pivots = jnp.sum(tile[:, :TILE] * eye, axis=1, keepdims=True)
                block = fine(tile[:, TILE:] * lax.rsqrt(pivots), work_ref[start:end, :])
                work_ref[start:end, :] = block
                if end < width:
                    work_ref[end:, :] = work_ref[end:, :] - fine(block[:, end:width], block, TN)
            inverse_ref[...] = work_ref[:, width:]

    shape = [((width, width), F32)] * 2
    return kernel_call(body, [mine, other], shape, [pltpu.VMEM((width, 2 * width), F32)])


def gather(cols, group, total, chunks, moved, last):
    width = chunks[0].shape[1]
    first = total is None
    flat = [] if first else [total]
    for c, (swapped, parts) in zip(group, moved):
        flat += [chunks[c], *swapped, *parts]

    def body(*refs):
        @pl.when(jnp.logical_not(at_root()))
        def _():
            ins, outs = list(refs[: len(flat)]), list(refs[len(flat) :])
            acc = None if first else ins.pop(0)[...]
            for c, (swapped, parts) in zip(group, moved):
                block = ins.pop(0)[...]
                hub = [ins.pop(0)[...] for _ in swapped]
                parts = [ins.pop(0)[...] for _ in parts]
                got = sum(parts[1:], parts[0])
                if hub:
                    got = jnp.where(lax.axis_index("col") == cols // 2 + 1 - c % 2, hub[0], got)
                pair = split(got)
                outs.pop(0)[...] = pair[0]
                outs.pop(0)[...] = pair[1]
                part = three(pair, split(block), TN)
                acc = part if acc is None else acc + part
            if last:
                halves(acc, *outs)
            else:
                outs[0][...] = acc

    shape = [(chunks[c].shape, BF16) for c in group for _ in range(2)]
    shape += [((width // 2, width), F32)] * 2 if last else [((width, width), F32)]
    return kernel_call(body, flat, shape)


def finish(inverse, gram, mine, other, chunks, sent, pairs):
    width = chunks[0].shape[1]
    rows = sum(c.shape[0] for c in chunks)
    at = cuts(rows)

    def body(own_ref, gram_ref, mine_ref, other_ref, *refs):
        blocks, refs = refs[:CHUNKS], refs[CHUNKS:]
        moved, refs = refs[: len(sent)], refs[len(sent) :]
        held, refs = refs[: 2 * CHUNKS], refs[2 * CHUNKS :]
        out_ref, projected_ref, buffer_ref, small_ref, sem = refs

        def store(value):
            small_ref[...] = value
            pltpu.make_async_copy(small_ref, projected_ref, sem.at[CHUNKS]).start()

        def put(c, value):
            there = pl.ds(at[c], at[c + 1] - at[c])
            buffer_ref[there, :] = value
            pltpu.make_async_copy(buffer_ref.at[there, :], out_ref.at[there, :], sem.at[c]).start()

        @pl.when(at_root())
        def _():
            store(fine(own_ref[...], gram_ref[...]))
            weight = split(own_ref[...].T)
            for c in range(CHUNKS):
                put(c, three(split(blocks[c][...]), weight))

        @pl.when(jnp.logical_not(at_root()))
        def _():
            parts = [ref[...] for ref in moved]
            got = sum(parts[1:], parts[0])
            projected = fine(got, joined(mine_ref[...], other_ref[...]))
            store(projected)
            weight = split(fine(got, projected, TN))
            for c in range(CHUNKS):
                put(c, blocks[c][...] - three((held[2 * c][...], held[2 * c + 1][...]), weight))

        for c in range(CHUNKS):
            there = pl.ds(at[c], at[c + 1] - at[c])
            pltpu.make_async_copy(buffer_ref.at[there, :], out_ref.at[there, :], sem.at[c]).wait()
        pltpu.make_async_copy(small_ref, projected_ref, sem.at[CHUNKS]).wait()

    return kernel_call(
        body,
        [inverse, gram, mine, other, *chunks, *sent, *pairs],
        [((rows, width), F32), ((width, width), F32)],
        [
            pltpu.VMEM((rows, width), F32),
            pltpu.VMEM((width, width), F32),
            pltpu.SemaphoreType.DMA((CHUNKS + 1,)),
        ],
        hbm_out=2,
        room=16,
    )


def added(values):
    def body(*refs):
        total = refs[0][...]
        for ref in refs[1:-1]:
            total = total + ref[...]
        refs[-1][...] = total

    return kernel_call(body, values, [(values[0].shape, F32)])[0]


def exchange(mine, send, rows, cols, members, two):
    def swap(part, bit):
        pairs = [(r * cols + c, (r ^ (bit if c in members else 1)) * cols + c) for r in range(rows) for c in range(cols)]
        return lax.ppermute(part, ("row", "col"), pairs)

    mine = added([mine, swap(send, 1)])
    bit = 2
    while bit < rows:
        bits = [bit, 2 * bit, 3 * bit] if two and 2 * bit < rows else [bit]
        mine = added([mine] + [swap(mine, b) for b in bits])
        bit *= 4 if len(bits) > 1 else 2
    return mine, swap(mine, 1)


def hop(value, pairs):
    return lax.ppermute(value, "col", pairs)


def outward(parts, cols):
    down, up = cols // 2 - 1, cols // 2 + 2
    while down > 1 or up + 1 < cols:
        pairs = ([(down, down - 1)] if down > 1 else []) + ([(up, up + 1)] if up + 1 < cols else [])
        parts.append(hop(parts[-1], pairs))
        down, up = down - 1, up + 1


def spread(chunks, cols):
    lower, upper = cols // 2, cols // 2 + 1
    if cols < 4:
        return [([], [hop(v, [(0, c)]) for c in range(1, cols)]) for v in chunks]
    parts = [[hop(v, [(0, upper if c % 2 else lower)])] for c, v in enumerate(chunks)]
    swaps = [[] for _ in chunks]
    for p in range(PAIRS + 1):
        here = [c for c in (2 * p, 2 * p + 1) if c < len(chunks)]
        for c in here:
            hub = upper if c % 2 else lower
            sides = [hop(parts[c][0], [(hub, lower - 1)])]
            if upper + 1 < cols:
                sides.append(hop(parts[c][0], [(hub, upper + 1)]))
                sides = [sum(sides[1:], sides[0])]
            parts[c] += sides
            outward(parts[c], cols)
        held = [parts[c][0] for c in here]
        pairs = [(lower, upper), (upper, lower)][: len(here)]
        swapped = hop(added(held) if len(held) > 1 else held[0], pairs)
        for c in here:
            swaps[c].append(swapped)
    return list(zip(swaps, parts))


def spread_last(value, cols):
    hub = max(cols // 2, 1)
    held = hop(value, [(0, hub)])
    parts = [held]
    ends = [(hub, hub - 1), (hub, hub + 1)]
    sides = [hop(held, [e]) for e in ends if 0 < e[1] < cols]
    parts += sides
    tail = sum(sides[1:], sides[0]) if sides else None
    down, up = hub - 1, hub + 1
    while down > 1 or up + 1 < cols:
        pairs = ([(down, down - 1)] if down > 1 else []) + ([(up, up + 1)] if up + 1 < cols else [])
        tail = hop(tail, pairs)
        parts.append(tail)
        down, up = down - 1, up + 1
    return parts


def solution(mesh):
    rows, cols = mesh.shape["row"], mesh.shape["col"]

    def per_device(columns):
        first = head(columns)
        *others, keep, send = rest(columns, first)
        chunks = [first, *others]
        moved = spread(chunks, cols)
        gram, inverse = factor(*exchange(keep, send, rows, cols, (0,), False))
        sent = spread_last(inverse, cols)
        total, pairs = None, []
        for group in GROUPS:
            got = gather(cols, group, total, chunks, [moved[c] for c in group], group == GROUPS[-1])
            pairs, total = [*pairs, *got[: 2 * len(group)]], got[2 * len(group)]
        total = exchange(*got[-2:], rows, cols, tuple(range(1, cols)), True)
        return tuple(finish(inverse, gram, *total, chunks, sent, pairs))

    return jax.shard_map(
        per_device, mesh=mesh, in_specs=(P("row", "col"),), out_specs=(P("row", "col"), P(None, "col")), check_vma=False
    )
```

```python
import jax
import jax.numpy as jnp
from jax import lax
from jax.experimental import pallas as pl
from jax.experimental.pallas import tpu as pltpu
from jax.sharding import PartitionSpec as P


CHUNKS = 11
GROUPS = ((0, 1, 2, 3), (4, 5, 6), (7, 8), (9,), (10,))
TILE = 64
F32 = jnp.float32
BF16 = jnp.bfloat16
VMEM = pl.BlockSpec(memory_space=pltpu.VMEM)
ANY = pl.BlockSpec(memory_space=pl.ANY)
NN = ((1,), (0,))
TN = ((0,), (0,))


def at_root():
    return lax.axis_index("col") == 0


def is_odd():
    return lax.axis_index("row") % 2 == 1


def kernel_call(body, operands, outputs, scratch=(), hbm_in=0, hbm_out=0, room=8):
    held = [pltpu.with_memory_space_constraint(o, pltpu.HBM) for o in operands[:hbm_in]]
    held += [pltpu.with_memory_space_constraint(o, pltpu.VMEM) for o in operands[hbm_in:]]
    shapes = [jax.ShapeDtypeStruct(s, d) for s, d in outputs[:hbm_out]]
    shapes += [pltpu.VMEM(s, d) for s, d in outputs[hbm_out:]]
    return pl.pallas_call(
        body,
        out_shape=tuple(shapes),
        in_specs=[ANY] * hbm_in + [VMEM] * (len(operands) - hbm_in),
        out_specs=tuple([ANY] * hbm_out + [VMEM] * (len(outputs) - hbm_out)),
        scratch_shapes=scratch,
        compiler_params=pltpu.CompilerParams(vmem_limit_bytes=room << 20),
    )(*held)


def fine(left, right, dims=NN):
    return lax.dot_general(left, right, (dims, ((), ())), precision=lax.Precision.HIGHEST, preferred_element_type=F32)


def split(value):
    high = value.astype(BF16)
    return high, (value - high.astype(F32)).astype(BF16)


def three(left, right, dims=NN):
    one = lambda a, b: lax.dot_general(a, b, (dims, ((), ())), preferred_element_type=F32)
    return one(left[0], right[0]) + (one(left[0], right[1]) + one(left[1], right[0]))


def halves(value, keep_ref, send_ref):
    half = value.shape[0] // 2
    odd = is_odd()
    keep_ref[...] = jnp.where(odd, value[half:], value[:half])
    send_ref[...] = jnp.where(odd, value[:half], value[half:])


def joined(mine, other):
    odd = is_odd()
    return jnp.concatenate([jnp.where(odd, other, mine), jnp.where(odd, mine, other)], axis=0)


def cuts(rows):
    step = -(-rows // (16 * CHUNKS)) * 16
    return [min(c * step, rows) for c in range(CHUNKS + 1)]


def fetch(columns_ref, refs, which, at, sem):
    copies = [
        pltpu.make_async_copy(columns_ref.at[at[c] : at[c + 1], :], ref, sem.at[k])
        for k, (c, ref) in enumerate(zip(which, refs))
    ]
    for copy in copies:
        copy.start()
    for copy in copies:
        copy.wait()


def head(columns):
    rows, width = columns.shape
    at = cuts(rows)

    def body(columns_ref, first_ref, second_ref, sem):
        @pl.when(at_root())
        def _():
            fetch(columns_ref, [first_ref, second_ref], [0, 1], at, sem)

    shape = [((at[c + 1] - at[c], width), F32) for c in (0, 1)]
    return kernel_call(body, [columns], shape, [pltpu.SemaphoreType.DMA((2,))], hbm_in=1)


def rest(columns):
    rows, width = columns.shape
    at = cuts(rows)

    def body(columns_ref, *refs):
        outs, (keep_ref, send_ref, sem) = refs[:CHUNKS], refs[CHUNKS:]
        fetch(columns_ref, outs, range(CHUNKS), at, sem)

        @pl.when(at_root())
        def _():
            total = None
            for ref in outs:
                pair = split(ref[...])
                part = three(pair, pair, TN)
                total = part if total is None else total + part
            halves(total, keep_ref, send_ref)

    shape = [((at[c + 1] - at[c], width), F32) for c in range(CHUNKS)] + [((width // 2, width), F32)] * 2
    return kernel_call(body, [columns], shape, [pltpu.SemaphoreType.DMA((CHUNKS,))], hbm_in=1)


def eliminate(tile, size):
    lanes = tile.shape[1]
    row = lax.broadcasted_iota(jnp.int32, (size, 1), 0)
    for j in range(0, size, 2):
        low = j // 8 * 8
        tail, at = tile[low:], row[low:]
        k, count = j - low, size - low
        c0 = jnp.broadcast_to(tail[:, j : j + 1], (count, lanes))
        c1 = jnp.broadcast_to(tail[:, j + 1 : j + 2], (count, lanes))
        p00, p01, p11 = c0[k : k + 1], c1[k : k + 1], c1[k + 1 : k + 2]
        r0, r1 = tail[k : k + 1], tail[k + 1 : k + 2]
        scale = 1.0 / (p00 * p11 - p01 * p01)
        q0 = (p11 * r0 - p01 * r1) * scale
        q1 = (p00 * r1 - p01 * r0) * scale
        inner = r0 * (p01 * (1.0 / p00))
        tail = tail - jnp.where(at > j + 1, c0 * q0 + c1 * q1, jnp.where(at == j + 1, inner, 0.0))
        tile = tail if low == 0 else jnp.concatenate([tile[:low], tail], axis=0)
    return tile


def identity(size):
    shape = (size, size)
    same = lax.broadcasted_iota(jnp.int32, shape, 0) == lax.broadcasted_iota(jnp.int32, shape, 1)
    return jnp.where(same, 1.0, 0.0).astype(F32)


def factor(mine, other):
    width = mine.shape[1]

    def body(mine_ref, other_ref, gram_ref, inverse_ref, half_ref, work_ref):
        @pl.when(at_root())
        def _():
            gram = joined(mine_ref[...], other_ref[...])
            gram_ref[...] = gram
            work_ref[:, :width] = gram
            work_ref[:, width:] = identity(width)
            eye = identity(TILE)
            for start in range(0, width, TILE):
                end = start + TILE
                tile = jnp.concatenate([work_ref[start:end, start:end], eye], axis=1)
                tile = eliminate(tile, TILE)
                pivots = jnp.sum(tile[:, :TILE] * eye, axis=1, keepdims=True)
                block = fine(tile[:, TILE:] * lax.rsqrt(pivots), work_ref[start:end, :])
                work_ref[start:end, :] = block
                if end < width:
                    work_ref[end:, :] = work_ref[end:, :] - fine(block[:, end:width], block, TN)
            inverse_ref[...] = work_ref[:, width:]
            half = width // 2
            half_ref[...] = jnp.where(is_odd(), work_ref[half:, width:], work_ref[:half, width:])

    shape = [((width, width), F32)] * 2 + [((width // 2, width), F32)]
    return kernel_call(body, [mine, other], shape, [pltpu.VMEM((width, 2 * width), F32)])


def gather(group, total, chunks, moved, last):
    width = chunks[0].shape[1]
    first = total is None
    flat = [] if first else [total]
    for c, (chosen, parts) in zip(group, moved):
        flat += [chunks[c], *chosen.values(), *parts]

    def body(*refs):
        @pl.when(jnp.logical_not(at_root()))
        def _():
            ins, outs = list(refs[: len(flat)]), list(refs[len(flat) :])
            acc = None if first else ins.pop(0)[...]
            for chosen, parts in moved:
                block = ins.pop(0)[...]
                hubs = [(where, ins.pop(0)[...]) for where in chosen]
                parts = [ins.pop(0)[...] for _ in parts]
                got = sum(parts[1:], parts[0])
                for where, value in hubs:
                    got = jnp.where(lax.axis_index("col") == where, value, got)
                pair = split(got)
                outs.pop(0)[...] = pair[0]
                outs.pop(0)[...] = pair[1]
                part = three(pair, split(block), TN)
                acc = part if acc is None else acc + part
            if last:
                halves(acc, *outs)
            else:
                outs[0][...] = acc

    shape = [(chunks[c].shape, BF16) for c in group for _ in range(2)]
    shape += [((width // 2, width), F32)] * 2 if last else [((width, width), F32)]
    return kernel_call(body, flat, shape)


def prepare(inverse, mine, other):
    shape = inverse.shape

    def body(own_ref, mine_ref, other_ref, factor_ref, square_ref):
        @pl.when(jnp.logical_not(at_root()))
        def _():
            got = joined(mine_ref[...], other_ref[...])
            factor_ref[...] = got
            square_ref[...] = fine(got, got, TN)

        @pl.when(at_root())
        def _():
            factor_ref[...] = own_ref[...]

    return kernel_call(body, [inverse, mine, other], [(shape, F32)] * 2)


def finish(factored, square, gram, mine, other, chunks, pairs):
    width = chunks[0].shape[1]
    rows = sum(c.shape[0] for c in chunks)
    at = cuts(rows)

    def body(factor_ref, square_ref, gram_ref, mine_ref, other_ref, *refs):
        blocks, refs = refs[:CHUNKS], refs[CHUNKS:]
        held, refs = refs[: 2 * CHUNKS], refs[2 * CHUNKS :]
        out_ref, projected_ref, buffer_ref, small_ref, sem = refs

        def store(value):
            small_ref[...] = value
            pltpu.make_async_copy(small_ref, projected_ref, sem.at[CHUNKS]).start()

        def put(c, value):
            there = pl.ds(at[c], at[c + 1] - at[c])
            buffer_ref[there, :] = value
            pltpu.make_async_copy(buffer_ref.at[there, :], out_ref.at[there, :], sem.at[c]).start()

        @pl.when(at_root())
        def _():
            weight = split(factor_ref[...].T)
            for c in range(CHUNKS):
                put(c, three(split(blocks[c][...]), weight))
            store(fine(factor_ref[...], gram_ref[...]))

        @pl.when(jnp.logical_not(at_root()))
        def _():
            total = joined(mine_ref[...], other_ref[...])
            weight = split(fine(square_ref[...], total))
            for c in range(CHUNKS):
                put(c, blocks[c][...] - three((held[2 * c][...], held[2 * c + 1][...]), weight))
            store(fine(factor_ref[...], total))

        for c in range(CHUNKS):
            there = pl.ds(at[c], at[c + 1] - at[c])
            pltpu.make_async_copy(buffer_ref.at[there, :], out_ref.at[there, :], sem.at[c]).wait()
        pltpu.make_async_copy(small_ref, projected_ref, sem.at[CHUNKS]).wait()

    return kernel_call(
        body,
        [factored, square, gram, mine, other, *chunks, *pairs],
        [((rows, width), F32), ((width, width), F32)],
        [
            pltpu.VMEM((rows, width), F32),
            pltpu.VMEM((width, width), F32),
            pltpu.SemaphoreType.DMA((CHUNKS + 1,)),
        ],
        hbm_out=2,
        room=16,
    )


def added(values):
    def body(*refs):
        total = refs[0][...]
        for ref in refs[1:-1]:
            total = total + ref[...]
        refs[-1][...] = total

    return kernel_call(body, values, [(values[0].shape, F32)])[0]


def swap(value, across, rows, cols, bit=0, members=()):
    pairs = []
    for r in range(rows):
        for c in range(cols):
            there = r * cols + across[c] if c in across else (r ^ (bit if c in members else 1)) * cols + c
            pairs.append((r * cols + c, there))
    return lax.ppermute(value, ("row", "col"), pairs)


def exchange(mine, send, rows, cols, members, two):
    get = lambda value, bit: swap(value, {}, rows, cols, bit, members)
    mine = added([mine, get(send, 1)])
    bit = 2
    while bit < rows:
        bits = [bit, 2 * bit, 3 * bit] if two and 2 * bit < rows else [bit]
        mine = added([mine] + [get(mine, b) for b in bits])
        bit *= 4 if len(bits) > 1 else 2
    return mine, get(mine, 1)


def hop(value, pairs):
    return lax.ppermute(value, "col", pairs)


def outward(parts, cols):
    down, up = cols // 2 - 1, cols // 2 + 1
    while down > 1 or up + 1 < cols:
        pairs = ([(down, down - 1)] if down > 1 else []) + ([(up, up + 1)] if up + 1 < cols else [])
        parts.append(hop(parts[-1], pairs))
        down, up = down - 1, up + 1


def direct(value, cols):
    middle = sorted(range(1, cols), key=lambda c: abs(c - cols // 2))
    return [hop(value, [(0, c)]) for c in middle]


def spread(chunks, rows, cols):
    hub = cols // 2
    if cols < 4:
        return [({}, [hop(v, [(0, c)]) for c in range(1, cols)]) for v in chunks]
    cycle = [(0, hub), *[(k, k + 1) for k in range(hub, cols - 1)], (cols - 1, hub - 1)]
    cycle += [(k, k - 1) for k in range(hub - 1, 0, -1)]
    moved = []
    for c, value in enumerate(chunks):
        got = hop(value, cycle if c < 2 else [(0, hub)])
        near = cols == 4 and c == len(chunks) - 1
        low = hop(value, [(0, hub - 1)]) if near else hop(got, [(hub, hub - 1)])
        high = swap(got, {hub: hub + 1, hub + 1: hub}, rows, cols)
        if cols == 4:
            moved.append(({hub: got, hub + 1: high}, [low]))
            continue
        parts = [jnp.where(lax.axis_index("col") == hub + 1, high, low)]
        outward(parts, cols)
        moved.append(({hub: got}, parts))
    return moved


def spread_last(value, cols):
    hub = max(cols // 2, 1)
    if cols <= 4:
        return direct(value, cols)
    held = hop(value, [(0, hub)])
    parts = [held]
    ends = [(hub, hub - 1), (hub, hub + 1)]
    sides = [hop(held, [e]) for e in ends if 0 < e[1] < cols]
    parts += sides
    tail = sum(sides[1:], sides[0]) if sides else None
    down, up = hub - 1, hub + 1
    while down > 1 or up + 1 < cols:
        pairs = ([(down, down - 1)] if down > 1 else []) + ([(up, up + 1)] if up + 1 < cols else [])
        tail = hop(tail, pairs)
        parts.append(tail)
        down, up = down - 1, up + 1
    return parts


def solution(mesh):
    rows, cols = mesh.shape["row"], mesh.shape["col"]

    def per_device(columns):
        *chunks, keep, send = rest(columns)
        moved = spread([*head(columns), *chunks[2:]], rows, cols)
        gram, inverse, half = factor(*exchange(keep, send, rows, cols, (0,), False))
        sent = added(spread_last(half, cols))
        sent = (sent, swap(sent, {}, rows, cols))
        total, pairs = None, []
        for group in GROUPS:
            got = gather(group, total, chunks, [moved[c] for c in group], group == GROUPS[-1])
            pairs, total = [*pairs, *got[: 2 * len(group)]], got[2 * len(group)]
        total = exchange(*got[-2:], rows, cols, tuple(range(1, cols)), True)
        return tuple(finish(*prepare(inverse, *sent), gram, *total, chunks, pairs))

    return jax.shard_map(
        per_device, mesh=mesh, in_specs=(P("row", "col"),), out_specs=(P("row", "col"), P(None, "col")), check_vma=False
    )
```

```python
import jax
import jax.numpy as jnp
from jax import lax
from jax.experimental import pallas as pl
from jax.experimental.pallas import tpu as pltpu
from jax.sharding import PartitionSpec as P


WEIGHTS = (12,) * 10 + (8,)
CHUNKS = len(WEIGHTS)
GROUPS = ((0, 1, 2, 3), (4, 5, 6), (7, 8), (9,), (10,))
TILE = 64
F32 = jnp.float32
BF16 = jnp.bfloat16
VMEM = pl.BlockSpec(memory_space=pltpu.VMEM)
ANY = pl.BlockSpec(memory_space=pl.ANY)
NN = ((1,), (0,))
TN = ((0,), (0,))


def at_root():
    return lax.axis_index("col") == 0


def is_odd():
    return lax.axis_index("row") % 2 == 1


def kernel_call(body, operands, outputs, scratch=(), hbm_in=0, hbm_out=0, room=8):
    held = [pltpu.with_memory_space_constraint(o, pltpu.HBM) for o in operands[:hbm_in]]
    held += [pltpu.with_memory_space_constraint(o, pltpu.VMEM) for o in operands[hbm_in:]]
    shapes = [jax.ShapeDtypeStruct(s, d) for s, d in outputs[:hbm_out]]
    shapes += [pltpu.VMEM(s, d) for s, d in outputs[hbm_out:]]
    return pl.pallas_call(
        body,
        out_shape=tuple(shapes),
        in_specs=[ANY] * hbm_in + [VMEM] * (len(operands) - hbm_in),
        out_specs=tuple([ANY] * hbm_out + [VMEM] * (len(outputs) - hbm_out)),
        scratch_shapes=scratch,
        compiler_params=pltpu.CompilerParams(vmem_limit_bytes=room << 20),
    )(*held)


def fine(left, right, dims=NN):
    return lax.dot_general(left, right, (dims, ((), ())), precision=lax.Precision.HIGHEST, preferred_element_type=F32)


def split(value):
    high = value.astype(BF16)
    return high, (value - high.astype(F32)).astype(BF16)


def three(left, right, dims=NN):
    one = lambda a, b: lax.dot_general(a, b, (dims, ((), ())), preferred_element_type=F32)
    return one(left[0], right[0]) + (one(left[0], right[1]) + one(left[1], right[0]))


def halves(value, keep_ref, send_ref):
    half = value.shape[0] // 2
    odd = is_odd()
    keep_ref[...] = jnp.where(odd, value[half:], value[:half])
    send_ref[...] = jnp.where(odd, value[:half], value[half:])


def joined(mine, other):
    odd = is_odd()
    return jnp.concatenate([jnp.where(odd, other, mine), jnp.where(odd, mine, other)], axis=0)


def cuts(rows):
    whole = sum(WEIGHTS)
    return [sum(WEIGHTS[:c]) * rows // whole // 16 * 16 for c in range(CHUNKS)] + [rows]


def fetch(columns_ref, refs, which, at, sem):
    copies = [
        pltpu.make_async_copy(columns_ref.at[at[c] : at[c + 1], :], ref, sem.at[k])
        for k, (c, ref) in enumerate(zip(which, refs))
    ]
    for copy in copies:
        copy.start()
    for copy in copies:
        copy.wait()


def head(columns):
    rows, width = columns.shape
    at = cuts(rows)

    def body(columns_ref, first_ref, second_ref, sem):
        @pl.when(at_root())
        def _():
            fetch(columns_ref, [first_ref, second_ref], [0, 1], at, sem)

    shape = [((at[c + 1] - at[c], width), F32) for c in (0, 1)]
    return kernel_call(body, [columns], shape, [pltpu.SemaphoreType.DMA((2,))], hbm_in=1)


def rest(columns):
    rows, width = columns.shape
    at = cuts(rows)

    def body(columns_ref, *refs):
        outs, (keep_ref, send_ref, sem) = refs[:CHUNKS], refs[CHUNKS:]
        fetch(columns_ref, outs, range(CHUNKS), at, sem)

        @pl.when(at_root())
        def _():
            total = None
            for ref in outs:
                pair = split(ref[...])
                part = three(pair, pair, TN)
                total = part if total is None else total + part
            halves(total, keep_ref, send_ref)

    shape = [((at[c + 1] - at[c], width), F32) for c in range(CHUNKS)] + [((width // 2, width), F32)] * 2
    return kernel_call(body, [columns], shape, [pltpu.SemaphoreType.DMA((CHUNKS,))], hbm_in=1)


def eliminate(tile, size):
    lanes = tile.shape[1]
    row = lax.broadcasted_iota(jnp.int32, (size, 1), 0)
    for j in range(0, size, 2):
        low = j // 8 * 8
        tail, at = tile[low:], row[low:]
        k, count = j - low, size - low
        c0 = jnp.broadcast_to(tail[:, j : j + 1], (count, lanes))
        c1 = jnp.broadcast_to(tail[:, j + 1 : j + 2], (count, lanes))
        p00, p01, p11 = c0[k : k + 1], c1[k : k + 1], c1[k + 1 : k + 2]
        r0, r1 = tail[k : k + 1], tail[k + 1 : k + 2]
        scale = 1.0 / (p00 * p11 - p01 * p01)
        q0 = (p11 * r0 - p01 * r1) * scale
        q1 = (p00 * r1 - p01 * r0) * scale
        inner = r0 * (p01 * (1.0 / p00))
        tail = tail - jnp.where(at > j + 1, c0 * q0 + c1 * q1, jnp.where(at == j + 1, inner, 0.0))
        tile = tail if low == 0 else jnp.concatenate([tile[:low], tail], axis=0)
    return tile


def identity(size):
    shape = (size, size)
    same = lax.broadcasted_iota(jnp.int32, shape, 0) == lax.broadcasted_iota(jnp.int32, shape, 1)
    return jnp.where(same, 1.0, 0.0).astype(F32)


def factor(mine, other):
    width = mine.shape[1]

    def body(mine_ref, other_ref, gram_ref, inverse_ref, half_ref, work_ref):
        @pl.when(at_root())
        def _():
            gram = joined(mine_ref[...], other_ref[...])
            gram_ref[...] = gram
            work_ref[:, :width] = gram
            work_ref[:, width:] = identity(width)
            eye = identity(TILE)
            for start in range(0, width, TILE):
                end = start + TILE
                tile = jnp.concatenate([work_ref[start:end, start:end], eye], axis=1)
                tile = eliminate(tile, TILE)
                pivots = jnp.sum(tile[:, :TILE] * eye, axis=1, keepdims=True)
                block = fine(tile[:, TILE:] * lax.rsqrt(pivots), work_ref[start:end, :])
                work_ref[start:end, :] = block
                if end < width:
                    work_ref[end:, :] = work_ref[end:, :] - fine(block[:, end:width], block, TN)
            inverse_ref[...] = work_ref[:, width:]
            half = width // 2
            half_ref[...] = jnp.where(is_odd(), work_ref[half:, width:], work_ref[:half, width:])

    shape = [((width, width), F32)] * 2 + [((width // 2, width), F32)]
    return kernel_call(body, [mine, other], shape, [pltpu.VMEM((width, 2 * width), F32)])


def gather(group, total, chunks, moved, last):
    width = chunks[0].shape[1]
    first = total is None
    flat = [] if first else [total]
    for c, (chosen, parts) in zip(group, moved):
        flat += [chunks[c], *chosen.values(), *parts]

    def body(*refs):
        @pl.when(jnp.logical_not(at_root()))
        def _():
            ins, outs = list(refs[: len(flat)]), list(refs[len(flat) :])
            acc = None if first else ins.pop(0)[...]
            for chosen, parts in moved:
                block = ins.pop(0)[...]
                hubs = [(where, ins.pop(0)[...]) for where in chosen]
                parts = [ins.pop(0)[...] for _ in parts]
                got = sum(parts[1:], parts[0])
                for where, value in hubs:
                    got = jnp.where(lax.axis_index("col") == where, value, got)
                pair = split(got)
                outs.pop(0)[...] = pair[0]
                outs.pop(0)[...] = pair[1]
                part = three(pair, split(block), TN)
                acc = part if acc is None else acc + part
            if last:
                halves(acc, *outs)
            else:
                outs[0][...] = acc

    shape = [(chunks[c].shape, BF16) for c in group for _ in range(2)]
    shape += [((width // 2, width), F32)] * 2 if last else [((width, width), F32)]
    return kernel_call(body, flat, shape)


def prepare(inverse, mine, other):
    shape = inverse.shape

    def body(own_ref, mine_ref, other_ref, factor_ref, square_ref):
        @pl.when(jnp.logical_not(at_root()))
        def _():
            got = joined(mine_ref[...], other_ref[...])
            factor_ref[...] = got
            square_ref[...] = fine(got, got, TN)

        @pl.when(at_root())
        def _():
            factor_ref[...] = own_ref[...]

    return kernel_call(body, [inverse, mine, other], [(shape, F32)] * 2)


def finish(factored, square, gram, mine, other, chunks, pairs):
    width = chunks[0].shape[1]
    rows = sum(c.shape[0] for c in chunks)
    at = cuts(rows)

    def body(factor_ref, square_ref, gram_ref, mine_ref, other_ref, *refs):
        blocks, refs = refs[:CHUNKS], refs[CHUNKS:]
        held, refs = refs[: 2 * CHUNKS], refs[2 * CHUNKS :]
        out_ref, projected_ref, buffer_ref, small_ref, sem = refs

        def store(value):
            small_ref[...] = value
            pltpu.make_async_copy(small_ref, projected_ref, sem.at[CHUNKS]).start()

        def put(c, value):
            there = pl.ds(at[c], at[c + 1] - at[c])
            buffer_ref[there, :] = value
            pltpu.make_async_copy(buffer_ref.at[there, :], out_ref.at[there, :], sem.at[c]).start()

        @pl.when(at_root())
        def _():
            weight = split(factor_ref[...].T)
            for c in range(CHUNKS):
                put(c, three(split(blocks[c][...]), weight))
            store(fine(factor_ref[...], gram_ref[...]))

        @pl.when(jnp.logical_not(at_root()))
        def _():
            total = joined(mine_ref[...], other_ref[...])
            weight = split(fine(square_ref[...], total))
            for c in range(CHUNKS):
                put(c, blocks[c][...] - three((held[2 * c][...], held[2 * c + 1][...]), weight))
            store(fine(factor_ref[...], total))

        for c in range(CHUNKS):
            there = pl.ds(at[c], at[c + 1] - at[c])
            pltpu.make_async_copy(buffer_ref.at[there, :], out_ref.at[there, :], sem.at[c]).wait()
        pltpu.make_async_copy(small_ref, projected_ref, sem.at[CHUNKS]).wait()

    return kernel_call(
        body,
        [factored, square, gram, mine, other, *chunks, *pairs],
        [((rows, width), F32), ((width, width), F32)],
        [
            pltpu.VMEM((rows, width), F32),
            pltpu.VMEM((width, width), F32),
            pltpu.SemaphoreType.DMA((CHUNKS + 1,)),
        ],
        hbm_out=2,
        room=16,
    )


def added(values):
    def body(*refs):
        total = refs[0][...]
        for ref in refs[1:-1]:
            total = total + ref[...]
        refs[-1][...] = total

    return kernel_call(body, values, [(values[0].shape, F32)])[0]


def swap(value, across, rows, cols, bit=0, members=()):
    pairs = []
    for r in range(rows):
        for c in range(cols):
            there = r * cols + across[c] if c in across else (r ^ (bit if c in members else 1)) * cols + c
            pairs.append((r * cols + c, there))
    return lax.ppermute(value, ("row", "col"), pairs)


def exchange(mine, send, rows, cols, members, two):
    get = lambda value, bit: swap(value, {}, rows, cols, bit, members)
    mine = added([mine, get(send, 1)])
    bit = 2
    while bit < rows:
        bits = [bit, 2 * bit, 3 * bit] if two and 2 * bit < rows else [bit]
        mine = added([mine] + [get(mine, b) for b in bits])
        bit *= 4 if len(bits) > 1 else 2
    return mine, get(mine, 1)


def hop(value, pairs):
    return lax.ppermute(value, "col", pairs)


def outward(parts, cols):
    down, up = cols // 2 - 1, cols // 2 + 1
    while down > 1 or up + 1 < cols:
        pairs = ([(down, down - 1)] if down > 1 else []) + ([(up, up + 1)] if up + 1 < cols else [])
        parts.append(hop(parts[-1], pairs))
        down, up = down - 1, up + 1


def direct(value, cols):
    middle = sorted(range(1, cols), key=lambda c: abs(c - cols // 2))
    return [hop(value, [(0, c)]) for c in middle]


def spread(chunks, rows, cols):
    hub = cols // 2
    if cols < 4:
        return [({}, [hop(v, [(0, c)]) for c in range(1, cols)]) for v in chunks]
    cycle = {0: hub, **{k: k - 1 for k in range(1, hub + 1)}}
    moved = []
    for c, value in enumerate(chunks):
        got = swap(value, cycle, rows, cols) if c < 2 else hop(value, [(0, hub)])
        near = cols == 4 and c == len(chunks) - 1
        low = hop(value, [(0, hub - 1)]) if near else hop(got, [(hub, hub - 1)])
        high = swap(got, {hub: hub + 1, hub + 1: hub}, rows, cols)
        if cols == 4:
            moved.append(({hub: got, hub + 1: high}, [low]))
            continue
        parts = [jnp.where(lax.axis_index("col") == hub + 1, high, low)]
        outward(parts, cols)
        moved.append(({hub: got}, parts))
    return moved


def spread_last(value, cols):
    hub = max(cols // 2, 1)
    if cols <= 4:
        return direct(value, cols)
    held = hop(value, [(0, hub)])
    parts = [held]
    ends = [(hub, hub - 1), (hub, hub + 1)]
    sides = [hop(held, [e]) for e in ends if 0 < e[1] < cols]
    parts += sides
    tail = sum(sides[1:], sides[0]) if sides else None
    down, up = hub - 1, hub + 1
    while down > 1 or up + 1 < cols:
        pairs = ([(down, down - 1)] if down > 1 else []) + ([(up, up + 1)] if up + 1 < cols else [])
        tail = hop(tail, pairs)
        parts.append(tail)
        down, up = down - 1, up + 1
    return parts


def solution(mesh):
    rows, cols = mesh.shape["row"], mesh.shape["col"]

    def per_device(columns):
        *chunks, keep, send = rest(columns)
        moved = spread([*head(columns), *chunks[2:]], rows, cols)
        gram, inverse, half = factor(*exchange(keep, send, rows, cols, (0,), False))
        sent = added(spread_last(half, cols))
        sent = (sent, swap(sent, {}, rows, cols))
        total, pairs = None, []
        for group in GROUPS:
            got = gather(group, total, chunks, [moved[c] for c in group], group == GROUPS[-1])
            pairs, total = [*pairs, *got[: 2 * len(group)]], got[2 * len(group)]
        total = exchange(*got[-2:], rows, cols, tuple(range(1, cols)), True)
        return tuple(finish(*prepare(inverse, *sent), gram, *total, chunks, pairs))

    return jax.shard_map(
        per_device, mesh=mesh, in_specs=(P("row", "col"),), out_specs=(P("row", "col"), P(None, "col")), check_vma=False
    )
```
